32 devices in a mesh: path: 8 (over z, core), fsdp: 4 (over y, x).
Axes of the slice: x: 2, y: 2, z: 4, core: 2. Of those that a mesh axis runs over, the one named last changes fastest.
Arguments:
- path_delta: bfloat16 [8, 4, 128, 4096], P('path', None, 'fsdp'), may hold values from -20 to 20
- feedback: float32 [8, 4, 128, 4096], P('path', None, 'fsdp'), may hold values from -4 to 4
- global_params: float32 [4, 2, 128, 4096], P(None, None, 'fsdp', 'path'), may hold values from -0.09375 to 0.09375
- momentum: float32 [4, 2, 128, 4096], P(None, None, 'fsdp', 'path'), may hold values from -2 to 2
- routes: int32 [8, 4], replicated, may hold values from 0 to 1
- token_counts: int32 [8, 4], replicated, may hold values from 1 to 16
- skip_flags: int32 [4, 2], replicated, may hold values from 0 to 1, as said below
Outputs:
- feedback_next: float32 [8, 4, 128, 4096], P('path', None, 'fsdp')
- momentum_next: float32 [4, 2, 128, 4096], P(None, None, 'fsdp', 'path')
- params_next: float32 [4, 2, 128, 4096], P(None, None, 'fsdp', 'path')
- path_params: bfloat16 [8, 4, 128, 4096], P('path', None, 'fsdp')
The draws below stay inside these ranges and needn't reach their ends.
Inputs may be any that keep to these rules, and one draw needn't show every extreme that they name: `skip_flags`: at most one of the two modules of a level skips.
All inputs are finite; a program needn't handle non-finite values.
Results may differ from the reference program's by a relative error of at most 0.012.
Values may be sent and summed in bfloat16 or wider, within the bound.
A program may use at most 64 MiB of HBM per device.

```python
import jax
import jax.numpy as jnp
from jax import lax

D = 4096
LEVELS = 4
PATHS = 8
PROWS = 128


def level_scale(key):
    quiet = jax.random.randint(jax.random.fold_in(key, 4242), (), 0, LEVELS)
    levels = jnp.arange(LEVELS, dtype=jnp.int32)
    return jnp.where(levels == quiet, 0.05, 1.0).astype(jnp.float32)[None, :, None, None]


def draw_path_delta(key, part):
    first_key = jax.random.fold_in(jax.random.fold_in(key, 17), 0)
    own = jax.random.truncated_normal(first_key, -4.0, 4.0, (PATHS, LEVELS, PROWS, D), jnp.float32)
    rowfrac = jnp.arange(PROWS, dtype=jnp.float32) / max(PROWS - 1, 1)
    colfrac = jnp.arange(D, dtype=jnp.float32) / (D - 1)
    scales = (1.0 + 2.0 * rowfrac)[:, None] * (1.0 + 2.0 * colfrac)[None, :] / 3.0
    mixed = own
    return jnp.clip(level_scale(key) * scales * mixed, -20.0, 20.0).astype(jnp.bfloat16)


def draw_feedback(key, part):
    values = jax.random.truncated_normal(jax.random.fold_in(key, 23), -8.0, 8.0, (PATHS, LEVELS, PROWS, D), jnp.float32)
    return jnp.clip(0.5 * level_scale(key) * values, -4.0, 4.0).astype(jnp.float32)


def draw_skip_flags(key, part):
    pattern = jax.random.randint(jax.random.fold_in(key, 31), (LEVELS,), 0, 3)
    first = (pattern == 0).astype(jnp.int32)
    second = (pattern == 1).astype(jnp.int32)
    return jnp.stack([first, second], axis=1)


def place_ends(drawn, stream_key, low, top_value):
    shape = drawn.shape
    place = [jax.random.randint(jax.random.fold_in(stream_key, axis), (), 0, shape[axis]) for axis in range(len(shape))]
    drawn = drawn.at[tuple(place)].set(low)
    longest = shape.index(max(shape))
    place[longest] = (place[longest] + 1) % shape[longest]
    return drawn.at[tuple(place)].set(top_value)


def block_scale(key, dims, shards, low, largest):
    factor_of, own = 1.0, jax.random.fold_in(key, 6)
    for dim, parts in shards:
        heights = jnp.exp(jax.random.uniform(jax.random.fold_in(own, dim), (parts,), jnp.float32, low / len(shards), largest / len(shards)))
        factor_of = factor_of * jnp.repeat(heights, dims[dim] // parts).reshape([-1 if axis == dim else 1 for axis in range(len(dims))])
    return factor_of


def normal_values(stream_key, shape, deviation, limit, pieces=(), held_as=jnp.bfloat16):
    drawn = jax.random.normal(stream_key, shape, jnp.float32) * deviation
    if len(pieces) > 0:
        drawn = block_scale(stream_key, shape, pieces, -0.22, 0.18) * drawn
    return jnp.clip(drawn, min=-limit, max=limit).astype(held_as)


def setup_inputs(seed: int = 0) -> dict:
    key_list = jax.random.split(jax.random.key(seed), 8)
    return {
        "path_delta": draw_path_delta(jax.random.fold_in(key_list[7], 71), 0),
        "feedback": draw_feedback(jax.random.fold_in(key_list[7], 71), 0),
        "global_params": normal_values(key_list[2], (LEVELS, 2, PROWS, D), D ** -0.5, 0.09375, ((2, 4), (3, 8)), jnp.float32),
        "momentum": normal_values(key_list[3], (LEVELS, 2, PROWS, D), 0.3, 2.0, ((2, 4), (3, 8)), jnp.float32),
        "routes": place_ends(jax.random.randint(key_list[4], (PATHS, LEVELS), 0, 2), jax.random.fold_in(key_list[4], 1), 0, 1).astype(jnp.int32),
        "token_counts": place_ends(jax.random.randint(key_list[5], (PATHS, LEVELS), 1, 17), jax.random.fold_in(key_list[5], 1), 1, 16).astype(jnp.int32),
        "skip_flags": draw_skip_flags(jax.random.fold_in(key_list[7], 71), 0),
    }


clip_rms = 0.2
outer_rate = 0.7
momentum_coef = 0.9
epsilon_sq = 1e-06

def reference(path_delta, feedback, global_params, momentum, routes, token_counts, skip_flags):
    counts = token_counts.astype(jnp.float32)
    same = (routes[:, None, :] == routes[None, :, :]).astype(jnp.float32)
    denom = lax.optimization_barrier(jnp.sum(same * counts[None, :, :], axis=1))
    weight = counts / denom
    skipped_path = jnp.where(routes == 1, skip_flags[None, :, 1], skip_flags[None, :, 0])
    live = (1 - skipped_path).astype(jnp.float32)
    feedback_parts = []
    average_parts = []
    for level in range(LEVELS):
        corrected = path_delta[:, level].astype(jnp.float32) + feedback[:, level]
        scaled = (weight[:, level, None, None] * corrected).astype(jnp.bfloat16)
        sent = jnp.where(live[:, level, None, None] > 0, scaled, jnp.zeros_like(scaled))
        sent_wide = sent.astype(jnp.float32)
        feedback_parts.append(corrected - live[:, level, None, None] * (sent_wide / weight[:, level, None, None]))
        upper = (routes[:, level] == 1).astype(jnp.float32)
        first = lax.optimization_barrier(jnp.sum((1.0 - upper)[:, None, None] * sent_wide, axis=0))
        second = lax.optimization_barrier(jnp.sum(upper[:, None, None] * sent_wide, axis=0))
        average_parts.append(jnp.stack([first, second]))
    feedback_next = jnp.stack(feedback_parts, axis=1)
    average = jnp.stack(average_parts)
    mean_sq = lax.optimization_barrier(jnp.mean(average * average, axis=(2, 3)))
    factor = jnp.minimum(1.0, clip_rms / jnp.sqrt(mean_sq + epsilon_sq))
    clipped = factor[:, :, None, None] * average
    skipped = (skip_flags > 0)[:, :, None, None]
    momentum_next = jnp.where(skipped, momentum, momentum_coef * momentum + clipped)
    params_next = jnp.where(skipped, global_params, global_params - outer_rate * (clipped + momentum_coef * momentum_next))
    narrow = params_next.astype(jnp.bfloat16)
    returned = []
    for level in range(LEVELS):
        pick = (routes[:, level] == 1)[:, None, None]
        returned.append(jnp.where(pick, narrow[level, 1][None], narrow[level, 0][None]))
    path_params = jnp.stack(returned, axis=1)
    return (feedback_next, momentum_next, params_next, path_params)
```

```python
import functools

import jax
import jax.numpy as jnp
from jax import lax
from jax.experimental import pallas as pl
from jax.experimental.pallas import tpu as pltpu
from jax.sharding import PartitionSpec as P

clip_rms = 0.2
outer_rate = 0.7
momentum_coef = 0.9
epsilon_sq = 1e-06
MESH = pl.DeviceIdType.MESH


def kernel(
    n, f,
    routes, counts, skips, delta_hbm, feed_hbm, params_hbm, mom_hbm,
    feed_out, mom_out, params_out, path_out,
    delta, feed, params, mom, sent, recv, average, chosen, gathered,
    square, square_in, part, part_in,
    load_sem, store_sem, send1, recv1, send2, recv2, sendf, recvf, sendp, recvp,
):
    levels, rows, depth = delta.shape
    cols = depth // n
    me = lax.axis_index("path")
    mf = lax.axis_index("fsdp")
    entries = rows * cols * n * f

    loads = []
    for l in range(levels):
        pair = (
            pltpu.make_async_copy(delta_hbm.at[0, l], delta.at[l], load_sem.at[0, l]),
            pltpu.make_async_copy(feed_hbm.at[0, l], feed.at[l], load_sem.at[1, l]),
        )
        for copy in pair:
            copy.start()
        loads.append(pair)
    load_params = pltpu.make_async_copy(params_hbm, params, load_sem.at[2, 0])
    load_mom = pltpu.make_async_copy(mom_hbm, mom, load_sem.at[3, 0])
    load_params.start()
    load_mom.start()

    barrier = pltpu.get_barrier_semaphore()
    for k in range(1, n):
        pl.semaphore_signal(barrier, inc=1, device_id={"path": lax.rem(me + k, n)}, device_id_type=MESH)
    for k in range(1, f):
        pl.semaphore_signal(barrier, inc=1, device_id={"fsdp": lax.rem(mf + k, f)}, device_id_type=MESH)

    inverse = []
    for l in range(levels):
        own_route = routes[me, l]
        total = jnp.int32(0)
        for q in range(n):
            total = total + jnp.where(routes[q, l] == own_route, counts[q, l], 0)
        live = 1 - jnp.where(own_route == 1, skips[l, 1], skips[l, 0])
        top = jnp.full((1, 128), (counts[me, l] * live).astype(jnp.float32))
        own = jnp.full((1, 128), counts[me, l].astype(jnp.float32))
        bottom = jnp.full((1, 128), total.astype(jnp.float32))
        weight = (top / bottom)[0:1, 0:1]
        inverse.append((bottom / own)[0:1, 0:1])
        for copy in loads[l]:
            copy.wait()
        for r in range(0, rows, 16):
            corrected = delta[l, r : r + 16, :].astype(jnp.float32) + feed[l, r : r + 16, :]
            sent[l, r : r + 16, :] = (weight * corrected).astype(jnp.bfloat16)
        if l == 0:
            pl.semaphore_wait(barrier, n - 1 + f - 1)
        for k in range(1, n):
            peer = lax.rem(me + k, n)
            pltpu.make_async_remote_copy(
                sent.at[l, :, pl.ds(pl.multiple_of(peer * cols, cols), cols)],
                recv.at[l, me],
                send1.at[l, k],
                recv1.at[l, me],
                device_id={"path": peer},
                device_id_type=MESH,
            ).start()

    stores = []
    for l in range(levels):
        for r in range(0, rows, 16):
            corrected = delta[l, r : r + 16, :].astype(jnp.float32) + feed[l, r : r + 16, :]
            feed[l, r : r + 16, :] = corrected - sent[l, r : r + 16, :].astype(jnp.float32) * inverse[l]
        copy = pltpu.make_async_copy(feed.at[l], feed_out.at[0, l], store_sem.at[0, l])
        copy.start()
        stores.append(copy)

    mine = pl.ds(pl.multiple_of(me * cols, cols), cols)

    def waiting1(l, k):
        source = lax.rem(me + k, n)
        return pltpu.make_async_remote_copy(
            sent.at[l, :, pl.ds(pl.multiple_of(source * cols, cols), cols)],
            recv.at[l, source], send1.at[l, k], recv1.at[l, source],
            device_id={"path": source}, device_id_type=MESH,
        )

    def small(l, k, axis, at, size, src, dst, send, arrive, slot):
        peer = lax.rem(at + k, size)
        return pltpu.make_async_remote_copy(
            src.at[l], dst.at[l, at if slot is None else peer], send.at[l, k],
            arrive.at[l, at if slot is None else peer],
            device_id={axis: peer}, device_id_type=MESH,
        )

    fsdp_copy = lambda l, k, slot: small(l, k, "fsdp", mf, f, square, square_in, sendf, recvf, slot)
    path_copy = lambda l, k, slot: small(l, k, "path", me, n, part, part_in, sendp, recvp, slot)

    def reduce_level(l):
        for k in range(1, n):
            waiting1(l, k).wait_recv()
        own = sent[l, :, mine].astype(jnp.float32)
        own_upper = routes[me, l] == 1
        zero = jnp.zeros_like(own)
        first = jnp.where(own_upper, zero, own)
        second = jnp.where(own_upper, own, zero)
        for k in range(1, n):
            source = lax.rem(me + k, n)
            upper = routes[source, l] == 1
            block = recv[l, source].astype(jnp.float32)
            first = first + jnp.where(upper, zero, block)
            second = second + jnp.where(upper, block, zero)
        for m, value in enumerate((first, second)):
            average[l, m] = value
            lanes = jnp.sum(value * value, axis=0, keepdims=True)
            folded = lanes[:, 0:128]
            for c in range(128, cols, 128):
                folded = folded + lanes[:, c : c + 128]
            square[l, m : m + 1, :] = folded
        for k in range(1, f):
            fsdp_copy(l, k, None).start()

    def share_level(l):
        total = square[l]
        for k in range(1, f):
            fsdp_copy(l, k, 1).wait_recv()
            total = total + square_in[l, lax.rem(mf + k, f)]
        part[l] = total
        for k in range(1, n):
            path_copy(l, k, None).start()

    def update_level(l):
        total = part[l]
        for k in range(1, n):
            path_copy(l, k, 1).wait_recv()
            total = total + part_in[l, lax.rem(me + k, n)]
        mean = jnp.sum(total, axis=1, keepdims=True) / entries
        factor = jnp.minimum(1.0, clip_rms / jnp.sqrt(mean + epsilon_sq))
        narrow = []
        for m in range(2):
            skipped = skips[l, m] > 0
            clipped = factor[m : m + 1, :] * average[l, m]
            momentum = mom[l, m]
            old = params[l, m]
            momentum = jnp.where(skipped, momentum, momentum_coef * momentum + clipped)
            new = jnp.where(skipped, old, old - outer_rate * (clipped + momentum_coef * momentum))
            mom[l, m] = momentum
            params[l, m] = new
            narrow.append(new.astype(jnp.bfloat16))
        for k in range(1, n):
            peer = lax.rem(me + k, n)
            chosen[l, k] = jnp.where(routes[peer, l] == 1, narrow[1], narrow[0])
            pltpu.make_async_remote_copy(
                chosen.at[l, k], gathered.at[l, :, mine], send2.at[l, k], recv2.at[l, me],
                device_id={"path": peer}, device_id_type=MESH,
            ).start()
        gathered[l, :, mine] = jnp.where(routes[me, l] == 1, narrow[1], narrow[0])
        for index, (src, dst) in enumerate(((mom, mom_out), (params, params_out))):
            copy = pltpu.make_async_copy(src.at[l], dst.at[l], store_sem.at[1 + index, l])
            copy.start()
            stores.append(copy)

    load_params.wait()
    load_mom.wait()
    for step in range(levels + 2):
        if step < levels:
            reduce_level(step)
        if 0 <= step - 1 < levels:
            share_level(step - 1)
        if 0 <= step - 2 < levels:
            update_level(step - 2)

    def waiting2(l, k):
        source = lax.rem(me + k, n)
        return pltpu.make_async_remote_copy(
            chosen.at[l, k], gathered.at[l, :, pl.ds(pl.multiple_of(source * cols, cols), cols)],
            send2.at[l, k], recv2.at[l, source], device_id={"path": source}, device_id_type=MESH,
        )

    for l in range(levels):
        for k in range(1, n):
            waiting2(l, k).wait_recv()
        copy = pltpu.make_async_copy(gathered.at[l], path_out.at[0, l], store_sem.at[3, l])
        copy.start()
        stores.append(copy)
    for l in range(levels):
        for k in range(1, n):
            waiting1(l, k).wait_send()
            waiting2(l, k).wait_send()
            path_copy(l, k, 1).wait_send()
        for k in range(1, f):
            fsdp_copy(l, k, 1).wait_send()
    for copy in stores:
        copy.wait()


def on_device(n, f, path_delta, feedback, global_params, momentum, routes, token_counts, skip_flags):
    _, levels, rows, depth = path_delta.shape
    cols = depth // n
    smem = pl.BlockSpec(memory_space=pltpu.SMEM)
    anywhere = pl.BlockSpec(memory_space=pl.ANY)
    shape = jax.ShapeDtypeStruct
    dma = pltpu.SemaphoreType.DMA
    bf16, f32 = jnp.bfloat16, jnp.float32
    return pl.pallas_call(
        functools.partial(kernel, n, f),
        out_shape=(
            shape(feedback.shape, f32),
            shape(momentum.shape, f32),
            shape(global_params.shape, f32),
            shape(path_delta.shape, bf16),
        ),
        in_specs=[smem] * 3 + [anywhere] * 4,
        out_specs=(anywhere,) * 4,
        scratch_shapes=[
            pltpu.VMEM((levels, rows, depth), bf16),
            pltpu.VMEM((levels, rows, depth), f32),
            pltpu.VMEM(global_params.shape, f32),
            pltpu.VMEM(global_params.shape, f32),
            pltpu.VMEM((levels, rows, depth), bf16),
            pltpu.VMEM((levels, n, rows, cols), bf16),
            pltpu.VMEM(global_params.shape, f32),
            pltpu.VMEM((levels, n, rows, cols), bf16),
            pltpu.VMEM((levels, rows, depth), bf16),
            pltpu.VMEM((levels, 2, 128), f32),
            pltpu.VMEM((levels, f, 2, 128), f32),
            pltpu.VMEM((levels, 2, 128), f32),
            pltpu.VMEM((levels, n, 2, 128), f32),
            dma((4, levels)),
            dma((4, levels)),
            dma((levels, n)),
            dma((levels, n)),
            dma((levels, n)),
            dma((levels, n)),
            dma((levels, f)),
            dma((levels, f)),
            dma((levels, n)),
            dma((levels, n)),
        ],
        compiler_params=pltpu.CompilerParams(collective_id=0, has_side_effects=True),
    )(routes, token_counts, skip_flags, path_delta, feedback, global_params, momentum)


def solution(mesh):
    return jax.shard_map(
        functools.partial(on_device, mesh.shape["path"], mesh.shape["fsdp"]),
        mesh=mesh,
        in_specs=(
            P("path", None, "fsdp", None),
            P("path", None, "fsdp", None),
            P(None, None, "fsdp", "path"),
            P(None, None, "fsdp", "path"),
            P(),
            P(),
            P(),
        ),
        out_specs=(
            P("path", None, "fsdp", None),
            P(None, None, "fsdp", "path"),
            P(None, None, "fsdp", "path"),
            P("path", None, "fsdp", None),
        ),
        check_vma=False,
    )
```

```python
import functools

import jax
import jax.numpy as jnp
from jax import lax
from jax.experimental import pallas as pl
from jax.experimental.pallas import tpu as pltpu
from jax.sharding import PartitionSpec as P

clip_rms = 0.2
outer_rate = 0.7
momentum_coef = 0.9
epsilon_sq = 1e-06
MESH = pl.DeviceIdType.MESH


def kernel(
    n, f,
    routes, counts, skips, delta_hbm, feed_hbm, params_hbm, mom_hbm,
    feed_out, mom_out, params_out, path_out,
    delta, feed, params, mom, sent, recv, average, blocks, gathered,
    square, square_in, part, part_in,
    load_sem, store_sem, send1, recv1, send_up, send_down, send_cross, recv2, sendf, recvf, sendp, recvp,
):
    levels, rows, depth = delta.shape
    cols = depth // n
    me = lax.axis_index("path")
    mf = lax.axis_index("fsdp")
    entries = rows * cols * n * f

    loads = []
    for l in range(levels):
        pair = (
            pltpu.make_async_copy(delta_hbm.at[0, l], delta.at[l], load_sem.at[0, l]),
            pltpu.make_async_copy(feed_hbm.at[0, l], feed.at[l], load_sem.at[1, l]),
        )
        for copy in pair:
            copy.start()
        loads.append(pair)
    load_params = pltpu.make_async_copy(params_hbm, params, load_sem.at[2, 0])
    load_mom = pltpu.make_async_copy(mom_hbm, mom, load_sem.at[3, 0])
    load_params.start()
    load_mom.start()

    barrier = pltpu.get_barrier_semaphore()
    for k in range(1, n):
        pl.semaphore_signal(barrier, inc=1, device_id={"path": lax.rem(me + k, n)}, device_id_type=MESH)
    for k in range(1, f):
        pl.semaphore_signal(barrier, inc=1, device_id={"fsdp": lax.rem(mf + k, f)}, device_id_type=MESH)

    inverse = []
    for l in range(levels):
        own_route = routes[l, me]
        total = jnp.int32(0)
        for q in range(n):
            total = total + jnp.where(routes[l, q] == own_route, counts[l, q], 0)
        live = 1 - jnp.where(own_route == 1, skips[1, l], skips[0, l])
        top = jnp.full((1, 128), (counts[l, me] * live).astype(jnp.float32))
        own = jnp.full((1, 128), counts[l, me].astype(jnp.float32))
        bottom = jnp.full((1, 128), total.astype(jnp.float32))
        weight = (top / bottom)[0:1, 0:1]
        inverse.append((bottom / own)[0:1, 0:1])
        for copy in loads[l]:
            copy.wait()
        for r in range(0, rows, 16):
            corrected = delta[l, r : r + 16, :].astype(jnp.float32) + feed[l, r : r + 16, :]
            sent[l, r : r + 16, :] = (weight * corrected).astype(jnp.bfloat16)
        if l == 0:
            pl.semaphore_wait(barrier, n - 1 + f - 1)
        for k in range(1, n):
            peer = lax.rem(me + k, n)
            pltpu.make_async_remote_copy(
                sent.at[l, :, pl.ds(pl.multiple_of(peer * cols, cols), cols)],
                recv.at[l, me],
                send1.at[l, k],
                recv1.at[l, me],
                device_id={"path": peer},
                device_id_type=MESH,
            ).start()

    stores = []
    for l in range(levels):
        for r in range(0, rows, 16):
            corrected = delta[l, r : r + 16, :].astype(jnp.float32) + feed[l, r : r + 16, :]
            feed[l, r : r + 16, :] = corrected - sent[l, r : r + 16, :].astype(jnp.float32) * inverse[l]
        copy = pltpu.make_async_copy(feed.at[l], feed_out.at[0, l], store_sem.at[0, l])
        copy.start()
        stores.append(copy)

    mine = pl.ds(pl.multiple_of(me * cols, cols), cols)

    def waiting1(l, k):
        source = lax.rem(me + k, n)
        return pltpu.make_async_remote_copy(
            sent.at[l, :, pl.ds(pl.multiple_of(source * cols, cols), cols)],
            recv.at[l, source], send1.at[l, k], recv1.at[l, source],
            device_id={"path": source}, device_id_type=MESH,
        )

    def small(l, k, axis, at, size, src, dst, send, arrive, slot):
        peer = lax.rem(at + k, size)
        return pltpu.make_async_remote_copy(
            src.at[l], dst.at[l, at if slot is None else peer], send.at[l, k],
            arrive.at[l, at if slot is None else peer],
            device_id={axis: peer}, device_id_type=MESH,
        )

    fsdp_copy = lambda l, k, slot: small(l, k, "fsdp", mf, f, square, square_in, sendf, recvf, slot)
    path_copy = lambda l, k, slot: small(l, k, "path", me, n, part, part_in, sendp, recvp, slot)

    def reduce_level(l):
        for k in range(1, n):
            waiting1(l, k).wait_recv()
        own = sent[l, :, mine].astype(jnp.float32)
        own_upper = routes[l, me] == 1
        zero = jnp.zeros_like(own)
        first = jnp.where(own_upper, zero, own)
        second = jnp.where(own_upper, own, zero)
        for k in range(1, n):
            source = lax.rem(me + k, n)
            upper = routes[l, source] == 1
            block = recv[l, source].astype(jnp.float32)
            first = first + jnp.where(upper, zero, block)
            second = second + jnp.where(upper, block, zero)
        for m, value in enumerate((first, second)):
            average[l, m] = value
            lanes = jnp.sum(value * value, axis=0, keepdims=True)
            folded = lanes[:, 0:128]
            for c in range(128, cols, 128):
                folded = folded + lanes[:, c : c + 128]
            square[l, m : m + 1, :] = folded
        for k in range(1, f):
            fsdp_copy(l, k, None).start()

    def share_level(l):
        total = square[l]
        for k in range(1, f):
            fsdp_copy(l, k, 1).wait_recv()
            total = total + square_in[l, lax.rem(mf + k, f)]
        part[l] = total
        for k in range(1, n):
            path_copy(l, k, None).start()

    z, core = lax.div(me, 2), lax.rem(me, 2)
    chips = n // 2

    def along_copy(l, owner, up):
        slot = 2 * owner + core
        return pltpu.make_async_remote_copy(
            blocks.at[l, slot], blocks.at[l, slot],
            (send_up if up else send_down).at[l, owner], recv2.at[l, slot],
            device_id={"path": me + 2 if up else me - 2}, device_id_type=MESH,
        )

    def cross_copy(l, owner):
        slot = 2 * owner + core
        return pltpu.make_async_remote_copy(
            blocks.at[l, slot], blocks.at[l, slot], send_cross.at[l, owner], recv2.at[l, slot],
            device_id={"path": me + 1 - 2 * core}, device_id_type=MESH,
        )

    def send_along(l, owner, up):
        @pl.when(z + 1 < chips if up else z > 0)
        def _():
            along_copy(l, owner, up).start()

    def arrived(l, slot):
        pltpu.make_async_remote_copy(
            blocks.at[l, slot], blocks.at[l, slot], send_cross.at[l, z], recv2.at[l, slot],
            device_id={"path": me + 1 - 2 * core}, device_id_type=MESH,
        ).wait_recv()

    def relay(l, d):
        @pl.when(z - d >= 0)
        def _():
            arrived(l, 2 * (z - d) + core)
            send_along(l, z - d, True)
            cross_copy(l, z - d).start()

        @pl.when(z + d < chips)
        def _():
            arrived(l, 2 * (z + d) + core)
            send_along(l, z + d, False)
            cross_copy(l, z + d).start()

    def finish_level(l):
        for owner in range(chips):
            arrived(l, 2 * owner + 1 - core)
        upper = routes[l, me] == 1
        for slot in range(n):
            gathered[l, :, slot * cols : (slot + 1) * cols] = jnp.where(upper, blocks[l, slot, 1], blocks[l, slot, 0])
        copy = pltpu.make_async_copy(gathered.at[l], path_out.at[0, l], store_sem.at[3, l])
        copy.start()
        stores.append(copy)

    def update_level(l):
        total = part[l]
        for k in range(1, n):
            path_copy(l, k, 1).wait_recv()
            total = total + part_in[l, lax.rem(me + k, n)]
        mean = jnp.sum(total, axis=1, keepdims=True) / entries
        factor = jnp.minimum(1.0, clip_rms / jnp.sqrt(mean + epsilon_sq))
        narrow = []
        for m in range(2):
            skipped = skips[m, l] > 0
            clipped = factor[m : m + 1, :] * average[l, m]
            momentum = mom[l, m]
            old = params[l, m]
            momentum = jnp.where(skipped, momentum, momentum_coef * momentum + clipped)
            new = jnp.where(skipped, old, old - outer_rate * (clipped + momentum_coef * momentum))
            mom[l, m] = momentum
            params[l, m] = new
            narrow.append(new.astype(jnp.bfloat16))
        for m in range(2):
            blocks[l, me, m] = narrow[m]
        send_along(l, z, True)
        send_along(l, z, False)
        cross_copy(l, z).start()
        for index, (src, dst) in enumerate(((mom, mom_out), (params, params_out))):
            copy = pltpu.make_async_copy(src.at[l], dst.at[l], store_sem.at[1 + index, l])
            copy.start()
            stores.append(copy)

    load_params.wait()
    load_mom.wait()
    for step in range(levels + 2 + chips):
        if step < levels:
            reduce_level(step)
        if 0 <= step - 1 < levels:
            share_level(step - 1)
        if 0 <= step - 2 < levels:
            update_level(step - 2)
        for d in range(1, chips):
            if 0 <= step - 2 - d < levels:
                relay(step - 2 - d, d)
        if 0 <= step - 2 - chips < levels:
            finish_level(step - 2 - chips)

    for l in range(levels):
        for k in range(1, n):
            waiting1(l, k).wait_send()
            path_copy(l, k, 1).wait_send()
        for k in range(1, f):
            fsdp_copy(l, k, 1).wait_send()
        for owner in range(chips):
            cross_copy(l, owner).wait_send()

            @pl.when((owner <= z) & (z + 1 < chips))
            def _():
                along_copy(l, owner, True).wait_send()

            @pl.when((owner >= z) & (z > 0))
            def _():
                along_copy(l, owner, False).wait_send()

    for copy in stores:
        copy.wait()


def on_device(n, f, path_delta, feedback, global_params, momentum, routes, token_counts, skip_flags):
    _, levels, rows, depth = path_delta.shape
    cols = depth // n
    smem = pl.BlockSpec(memory_space=pltpu.SMEM)
    anywhere = pl.BlockSpec(memory_space=pl.ANY)
    shape = jax.ShapeDtypeStruct
    dma = pltpu.SemaphoreType.DMA
    bf16, f32 = jnp.bfloat16, jnp.float32
    return pl.pallas_call(
        functools.partial(kernel, n, f),
        out_shape=(
            shape(feedback.shape, f32),
            shape(momentum.shape, f32),
            shape(global_params.shape, f32),
            shape(path_delta.shape, bf16),
        ),
        in_specs=[smem] * 3 + [anywhere] * 4,
        out_specs=(anywhere,) * 4,
        scratch_shapes=[
            pltpu.VMEM((levels, rows, depth), bf16),
            pltpu.VMEM((levels, rows, depth), f32),
            pltpu.VMEM(global_params.shape, f32),
            pltpu.VMEM(global_params.shape, f32),
            pltpu.VMEM((levels, rows, depth), bf16),
            pltpu.VMEM((levels, n, rows, cols), bf16),
            pltpu.VMEM(global_params.shape, f32),
            pltpu.VMEM((levels, n, 2, rows, cols), bf16),
            pltpu.VMEM((levels, rows, depth), bf16),
            pltpu.VMEM((levels, 2, 128), f32),
            pltpu.VMEM((levels, f, 2, 128), f32),
            pltpu.VMEM((levels, 2, 128), f32),
            pltpu.VMEM((levels, n, 2, 128), f32),
            dma((4, levels)),
            dma((4, levels)),
            dma((levels, n)),
            dma((levels, n)),
            dma((levels, n // 2)),
            dma((levels, n // 2)),
            dma((levels, n // 2)),
            dma((levels, n)),
            dma((levels, f)),
            dma((levels, f)),
            dma((levels, n)),
            dma((levels, n)),
        ],
        compiler_params=pltpu.CompilerParams(collective_id=0, has_side_effects=True),
    )(routes.T, token_counts.T, skip_flags.T, path_delta, feedback, global_params, momentum)


def solution(mesh):
    return jax.shard_map(
        functools.partial(on_device, mesh.shape["path"], mesh.shape["fsdp"]),
        mesh=mesh,
        in_specs=(
            P("path", None, "fsdp", None),
            P("path", None, "fsdp", None),
            P(None, None, "fsdp", "path"),
            P(None, None, "fsdp", "path"),
            P(),
            P(),
            P(),
        ),
        out_specs=(
            P("path", None, "fsdp", None),
            P(None, None, "fsdp", "path"),
            P(None, None, "fsdp", "path"),
            P("path", None, "fsdp", None),
        ),
        check_vma=False,
    )
```

```python
import functools

import jax
import jax.numpy as jnp
from jax import lax
from jax.experimental import pallas as pl
from jax.experimental.pallas import tpu as pltpu
from jax.sharding import PartitionSpec as P

clip_rms = 0.2
outer_rate = 0.7
momentum_coef = 0.9
epsilon_sq = 1e-06
MESH = pl.DeviceIdType.MESH
ahead = 2


def kernel(
    n, f,
    routes, counts, skips, delta_hbm, feed_hbm, params_hbm, mom_hbm,
    feed_out, mom_out, params_out, path_out,
    delta, feed, params, mom, sent, recv, average, blocks, gathered,
    square, square_in, part, part_in,
    load_sem, store_sem, send1, recv1, send_up, send_down, send_cross, recv2, sendf, recvf, sendp, recvp,
):
    levels, rows, depth = delta.shape
    cols = depth // n
    me = lax.axis_index("path")
    mf = lax.axis_index("fsdp")
    entries = rows * cols * n * f

    loads = []
    for l in range(levels):
        pair = (
            pltpu.make_async_copy(delta_hbm.at[0, l], delta.at[l], load_sem.at[0, l]),
            pltpu.make_async_copy(feed_hbm.at[0, l], feed.at[l], load_sem.at[1, l]),
        )
        for copy in pair:
            copy.start()
        loads.append(pair)
    load_params = pltpu.make_async_copy(params_hbm, params, load_sem.at[2, 0])
    load_mom = pltpu.make_async_copy(mom_hbm, mom, load_sem.at[3, 0])
    load_params.start()
    load_mom.start()

    barrier = pltpu.get_barrier_semaphore()
    for k in range(1, n):
        pl.semaphore_signal(barrier, inc=1, device_id={"path": lax.rem(me + k, n)}, device_id_type=MESH)
    for k in range(1, f):
        pl.semaphore_signal(barrier, inc=1, device_id={"fsdp": lax.rem(mf + k, f)}, device_id_type=MESH)

    inverse = []
    stores = []

    def send_level(l):
        own_route = routes[l, me]
        total = jnp.int32(0)
        for q in range(n):
            total = total + jnp.where(routes[l, q] == own_route, counts[l, q], 0)
        live = 1 - jnp.where(own_route == 1, skips[1, l], skips[0, l])
        top = jnp.full((1, 128), (counts[l, me] * live).astype(jnp.float32))
        own = jnp.full((1, 128), counts[l, me].astype(jnp.float32))
        bottom = jnp.full((1, 128), total.astype(jnp.float32))
        weight = (top / bottom)[0:1, 0:1]
        inverse.append((bottom / own)[0:1, 0:1])
        for copy in loads[l]:
            copy.wait()
        for r in range(0, rows, 16):
            corrected = delta[l, r : r + 16, :].astype(jnp.float32) + feed[l, r : r + 16, :]
            sent[l, r : r + 16, :] = (weight * corrected).astype(jnp.bfloat16)
        if l == 0:
            pl.semaphore_wait(barrier, n - 1 + f - 1)
        for k in range(1, n):
            peer = lax.rem(me + k, n)
            pltpu.make_async_remote_copy(
                sent.at[l, :, pl.ds(pl.multiple_of(peer * cols, cols), cols)],
                recv.at[l, me],
                send1.at[l, k],
                recv1.at[l, me],
                device_id={"path": peer},
                device_id_type=MESH,
            ).start()

    def feedback_level(l):
        for r in range(0, rows, 16):
            corrected = delta[l, r : r + 16, :].astype(jnp.float32) + feed[l, r : r + 16, :]
            feed[l, r : r + 16, :] = corrected - sent[l, r : r + 16, :].astype(jnp.float32) * inverse[l]
        copy = pltpu.make_async_copy(feed.at[l], feed_out.at[0, l], store_sem.at[0, l])
        copy.start()
        stores.append(copy)

    mine = pl.ds(pl.multiple_of(me * cols, cols), cols)

    def waiting1(l, k):
        source = lax.rem(me + k, n)
        return pltpu.make_async_remote_copy(
            sent.at[l, :, pl.ds(pl.multiple_of(source * cols, cols), cols)],
            recv.at[l, source], send1.at[l, k], recv1.at[l, source],
            device_id={"path": source}, device_id_type=MESH,
        )

    def small(l, k, axis, at, size, src, dst, send, arrive, slot):
        peer = lax.rem(at + k, size)
        return pltpu.make_async_remote_copy(
            src.at[l], dst.at[l, at if slot is None else peer], send.at[l, k],
            arrive.at[l, at if slot is None else peer],
            device_id={axis: peer}, device_id_type=MESH,
        )

    fsdp_copy = lambda l, k, slot: small(l, k, "fsdp", mf, f, square, square_in, sendf, recvf, slot)
    path_copy = lambda l, k, slot: small(l, k, "path", me, n, part, part_in, sendp, recvp, slot)

    def reduce_level(l):
        for k in range(1, n):
            waiting1(l, k).wait_recv()
        own = sent[l, :, mine].astype(jnp.float32)
        own_upper = routes[l, me] == 1
        zero = jnp.zeros_like(own)
        first = jnp.where(own_upper, zero, own)
        second = jnp.where(own_upper, own, zero)
        for k in range(1, n):
            source = lax.rem(me + k, n)
            upper = routes[l, source] == 1
            block = recv[l, source].astype(jnp.float32)
            first = first + jnp.where(upper, zero, block)
            second = second + jnp.where(upper, block, zero)
        for m, value in enumerate((first, second)):
            average[l, m] = value
            lanes = jnp.sum(value * value, axis=0, keepdims=True)
            folded = lanes[:, 0:128]
            for c in range(128, cols, 128):
                folded = folded + lanes[:, c : c + 128]
            square[l, m : m + 1, :] = folded
        for k in range(1, f):
            fsdp_copy(l, k, None).start()

    def share_level(l):
        total = square[l]
        for k in range(1, f):
            fsdp_copy(l, k, 1).wait_recv()
            total = total + square_in[l, lax.rem(mf + k, f)]
        part[l] = total
        for k in range(1, n):
            path_copy(l, k, None).start()

    z, core = lax.div(me, 2), lax.rem(me, 2)
    chips = n // 2

    def along_copy(l, owner, up):
        slot = 2 * owner + core
        return pltpu.make_async_remote_copy(
            blocks.at[l, slot], blocks.at[l, slot],
            (send_up if up else send_down).at[l, owner], recv2.at[l, slot],
            device_id={"path": me + 2 if up else me - 2}, device_id_type=MESH,
        )

    def cross_copy(l, owner):
        slot = 2 * owner + core
        return pltpu.make_async_remote_copy(
            blocks.at[l, slot], blocks.at[l, slot], send_cross.at[l, owner], recv2.at[l, slot],
            device_id={"path": me + 1 - 2 * core}, device_id_type=MESH,
        )

    def send_along(l, owner, up):
        @pl.when(z + 1 < chips if up else z > 0)
        def _():
            along_copy(l, owner, up).start()

    def arrived(l, slot):
        pltpu.make_async_remote_copy(
            blocks.at[l, slot], blocks.at[l, slot], send_cross.at[l, z], recv2.at[l, slot],
            device_id={"path": me + 1 - 2 * core}, device_id_type=MESH,
        ).wait_recv()

    def relay(l, d):
        @pl.when(z - d >= 0)
        def _():
            arrived(l, 2 * (z - d) + core)
            send_along(l, z - d, True)
            cross_copy(l, z - d).start()

        @pl.when(z + d < chips)
        def _():
            arrived(l, 2 * (z + d) + core)
            send_along(l, z + d, False)
            cross_copy(l, z + d).start()

    def finish_level(l):
        for owner in range(chips):
            arrived(l, 2 * owner + 1 - core)
        upper = routes[l, me] == 1
        for slot in range(n):
            gathered[l, :, slot * cols : (slot + 1) * cols] = jnp.where(upper, blocks[l, slot, 1], blocks[l, slot, 0])
        copy = pltpu.make_async_copy(gathered.at[l], path_out.at[0, l], store_sem.at[3, l])
        copy.start()
        stores.append(copy)

    def update_level(l):
        total = part[l]
        for k in range(1, n):
            path_copy(l, k, 1).wait_recv()
            total = total + part_in[l, lax.rem(me + k, n)]
        mean = jnp.sum(total, axis=1, keepdims=True) / entries
        factor = jnp.minimum(1.0, clip_rms / jnp.sqrt(mean + epsilon_sq))
        narrow = []
        for m in range(2):
            skipped = skips[m, l] > 0
            clipped = factor[m : m + 1, :] * average[l, m]
            momentum = mom[l, m]
            old = params[l, m]
            momentum = jnp.where(skipped, momentum, momentum_coef * momentum + clipped)
            new = jnp.where(skipped, old, old - outer_rate * (clipped + momentum_coef * momentum))
            mom[l, m] = momentum
            params[l, m] = new
            narrow.append(new.astype(jnp.bfloat16))
        for m in range(2):
            blocks[l, me, m] = narrow[m]
        send_along(l, z, True)
        send_along(l, z, False)
        cross_copy(l, z).start()
        for index, (src, dst) in enumerate(((mom, mom_out), (params, params_out))):
            copy = pltpu.make_async_copy(src.at[l], dst.at[l], store_sem.at[1 + index, l])
            copy.start()
            stores.append(copy)

    for l in range(min(ahead, levels)):
        send_level(l)
    for l in range(min(ahead, levels)):
        feedback_level(l)
    load_params.wait()
    load_mom.wait()
    for step in range(levels + 1 + chips):
        if step < levels:
            reduce_level(step)
            share_level(step)
            if step + ahead < levels:
                send_level(step + ahead)
                feedback_level(step + ahead)
        if 0 <= step - 1 < levels:
            update_level(step - 1)
        for d in range(1, chips):
            if 0 <= step - 1 - d < levels:
                relay(step - 1 - d, d)
        if 0 <= step - 1 - chips < levels:
            finish_level(step - 1 - chips)

    for l in range(levels):
        for k in range(1, n):
            waiting1(l, k).wait_send()
            path_copy(l, k, 1).wait_send()
        for k in range(1, f):
            fsdp_copy(l, k, 1).wait_send()
        for owner in range(chips):
            cross_copy(l, owner).wait_send()

            @pl.when((owner <= z) & (z + 1 < chips))
            def _():
                along_copy(l, owner, True).wait_send()

            @pl.when((owner >= z) & (z > 0))
            def _():
                along_copy(l, owner, False).wait_send()

    for copy in stores:
        copy.wait()


def on_device(n, f, path_delta, feedback, global_params, momentum, routes, token_counts, skip_flags):
    _, levels, rows, depth = path_delta.shape
    cols = depth // n
    smem = pl.BlockSpec(memory_space=pltpu.SMEM)
    anywhere = pl.BlockSpec(memory_space=pl.ANY)
    shape = jax.ShapeDtypeStruct
    dma = pltpu.SemaphoreType.DMA
    bf16, f32 = jnp.bfloat16, jnp.float32
    return pl.pallas_call(
        functools.partial(kernel, n, f),
        out_shape=(
            shape(feedback.shape, f32),
            shape(momentum.shape, f32),
            shape(global_params.shape, f32),
            shape(path_delta.shape, bf16),
        ),
        in_specs=[smem] * 3 + [anywhere] * 4,
        out_specs=(anywhere,) * 4,
        scratch_shapes=[
            pltpu.VMEM((levels, rows, depth), bf16),
            pltpu.VMEM((levels, rows, depth), f32),
            pltpu.VMEM(global_params.shape, f32),
            pltpu.VMEM(global_params.shape, f32),
            pltpu.VMEM((levels, rows, depth), bf16),
            pltpu.VMEM((levels, n, rows, cols), bf16),
            pltpu.VMEM(global_params.shape, f32),
            pltpu.VMEM((levels, n, 2, rows, cols), bf16),
            pltpu.VMEM((levels, rows, depth), bf16),
            pltpu.VMEM((levels, 2, 128), f32),
            pltpu.VMEM((levels, f, 2, 128), f32),
            pltpu.VMEM((levels, 2, 128), f32),
            pltpu.VMEM((levels, n, 2, 128), f32),
            dma((4, levels)),
            dma((4, levels)),
            dma((levels, n)),
            dma((levels, n)),
            dma((levels, n // 2)),
            dma((levels, n // 2)),
            dma((levels, n // 2)),
            dma((levels, n)),
            dma((levels, f)),
            dma((levels, f)),
            dma((levels, n)),
            dma((levels, n)),
        ],
        compiler_params=pltpu.CompilerParams(collective_id=0, has_side_effects=True),
    )(routes.T, token_counts.T, skip_flags.T, path_delta, feedback, global_params, momentum)


def solution(mesh):
    return jax.shard_map(
        functools.partial(on_device, mesh.shape["path"], mesh.shape["fsdp"]),
        mesh=mesh,
        in_specs=(
            P("path", None, "fsdp", None),
            P("path", None, "fsdp", None),
            P(None, None, "fsdp", "path"),
            P(None, None, "fsdp", "path"),
            P(),
            P(),
            P(),
        ),
        out_specs=(
            P("path", None, "fsdp", None),
            P(None, None, "fsdp", "path"),
            P(None, None, "fsdp", "path"),
            P("path", None, "fsdp", None),
        ),
        check_vma=False,
    )
```

```python
import functools

import jax
import jax.numpy as jnp
from jax import lax
from jax.experimental import pallas as pl
from jax.experimental.pallas import tpu as pltpu
from jax.sharding import PartitionSpec as P

clip_rms = 0.2
outer_rate = 0.7
momentum_coef = 0.9
epsilon_sq = 1e-06
MESH = pl.DeviceIdType.MESH
ahead = 2


def kernel(
    n, f,
    routes, counts, skips, delta_hbm, feed_hbm, params_hbm, mom_hbm,
    feed_out, mom_out, params_out, path_out,
    delta, feed, params, mom, sent, recv, average, blocks, gathered,
    square, square_in, part, part_in,
    load_sem, store_sem, send1, recv1, send_up, send_down, send_cross, recv2, sendf, recvf, sendp, recvp,
):
    levels, rows, depth = delta.shape
    cols = depth // n
    me = lax.axis_index("path")
    mf = lax.axis_index("fsdp")
    entries = rows * cols * n * f

    loads = []
    for l in range(levels):
        pair = (
            pltpu.make_async_copy(delta_hbm.at[0, l], delta.at[l], load_sem.at[0, l]),
            pltpu.make_async_copy(feed_hbm.at[0, l], feed.at[l], load_sem.at[1, l]),
        )
        for copy in pair:
            copy.start()
        loads.append(pair)
    load_params = pltpu.make_async_copy(params_hbm, params, load_sem.at[2, 0])
    load_mom = pltpu.make_async_copy(mom_hbm, mom, load_sem.at[3, 0])
    load_params.start()
    load_mom.start()

    barrier = pltpu.get_barrier_semaphore()
    for k in range(1, n):
        pl.semaphore_signal(barrier, inc=1, device_id={"path": lax.rem(me + k, n)}, device_id_type=MESH)
    for k in range(1, f):
        pl.semaphore_signal(barrier, inc=1, device_id={"fsdp": lax.rem(mf + k, f)}, device_id_type=MESH)

    inverse = []
    stores = []

    def send_level(l):
        own_route = routes[l, me]
        total = jnp.int32(0)
        for q in range(n):
            total = total + jnp.where(routes[l, q] == own_route, counts[l, q], 0)
        live = 1 - jnp.where(own_route == 1, skips[1, l], skips[0, l])
        top = jnp.full((1, 128), (counts[l, me] * live).astype(jnp.float32))
        own = jnp.full((1, 128), counts[l, me].astype(jnp.float32))
        bottom = jnp.full((1, 128), total.astype(jnp.float32))
        weight = (top / bottom)[0:1, 0:1]
        inverse.append((bottom / own)[0:1, 0:1])
        for copy in loads[l]:
            copy.wait()
        for r in range(0, rows, 16):
            corrected = delta[l, r : r + 16, :].astype(jnp.float32) + feed[l, r : r + 16, :]
            sent[l, r : r + 16, :] = (weight * corrected).astype(jnp.bfloat16)
        if l == 0:
            pl.semaphore_wait(barrier, n - 1 + f - 1)
        for k in range(1, n):
            peer = lax.rem(me + k, n)
            pltpu.make_async_remote_copy(
                sent.at[l, :, pl.ds(pl.multiple_of(peer * cols, cols), cols)],
                recv.at[l, me],
                send1.at[l, k],
                recv1.at[l, me],
                device_id={"path": peer},
                device_id_type=MESH,
            ).start()

    def feedback_level(l):
        for r in range(0, rows, 16):
            corrected = delta[l, r : r + 16, :].astype(jnp.float32) + feed[l, r : r + 16, :]
            feed[l, r : r + 16, :] = corrected - sent[l, r : r + 16, :].astype(jnp.float32) * inverse[l]
        copy = pltpu.make_async_copy(feed.at[l], feed_out.at[0, l], store_sem.at[0, l])
        copy.start()
        stores.append(copy)

    mine = pl.ds(pl.multiple_of(me * cols, cols), cols)

    def waiting1(l, k):
        source = lax.rem(me + k, n)
        return pltpu.make_async_remote_copy(
            sent.at[l, :, pl.ds(pl.multiple_of(source * cols, cols), cols)],
            recv.at[l, source], send1.at[l, k], recv1.at[l, source],
            device_id={"path": source}, device_id_type=MESH,
        )

    def small(l, k, axis, at, size, src, dst, send, arrive, slot):
        peer = lax.rem(at + k, size)
        return pltpu.make_async_remote_copy(
            src.at[l], dst.at[l, at if slot is None else peer], send.at[l, k],
            arrive.at[l, at if slot is None else peer],
            device_id={axis: peer}, device_id_type=MESH,
        )

    fsdp_copy = lambda l, k, slot: small(l, k, "fsdp", mf, f, square, square_in, sendf, recvf, slot)
    path_copy = lambda l, k, slot: small(l, k, "path", me, n, part, part_in, sendp, recvp, slot)

    def reduce_level(l):
        for k in range(1, n):
            waiting1(l, k).wait_recv()
        own = sent[l, :, mine].astype(jnp.float32)
        own_upper = routes[l, me] == 1
        zero = jnp.zeros_like(own)
        first = jnp.where(own_upper, zero, own)
        second = jnp.where(own_upper, own, zero)
        for k in range(1, n):
            source = lax.rem(me + k, n)
            upper = routes[l, source] == 1
            block = recv[l, source].astype(jnp.float32)
            first = first + jnp.where(upper, zero, block)
            second = second + jnp.where(upper, block, zero)
        for m, value in enumerate((first, second)):
            average[l, m] = value
            lanes = jnp.sum(value * value, axis=0, keepdims=True)
            folded = lanes[:, 0:128]
            for c in range(128, cols, 128):
                folded = folded + lanes[:, c : c + 128]
            square[l, m : m + 1, :] = folded
        for k in range(1, f):
            fsdp_copy(l, k, None).start()

    def share_level(l):
        total = square[l]
        for k in range(1, f):
            fsdp_copy(l, k, 1).wait_recv()
            total = total + square_in[l, lax.rem(mf + k, f)]
        part[l] = total
        for k in range(1, n):
            path_copy(l, k, None).start()

    z, core = lax.div(me, 2), lax.rem(me, 2)
    chips = n // 2

    def along_copy(l, owner, up):
        slot = 2 * owner + core
        return pltpu.make_async_remote_copy(
            blocks.at[l, slot], blocks.at[l, slot],
            (send_up if up else send_down).at[l, owner], recv2.at[l, slot],
            device_id={"path": me + 2 if up else me - 2}, device_id_type=MESH,
        )

    def cross_copy(l, owner):
        slot = 2 * owner + core
        return pltpu.make_async_remote_copy(
            blocks.at[l, slot], blocks.at[l, slot], send_cross.at[l, owner], recv2.at[l, slot],
            device_id={"path": me + 1 - 2 * core}, device_id_type=MESH,
        )

    def send_along(l, owner, up):
        @pl.when(z + 1 < chips if up else z > 0)
        def _():
            along_copy(l, owner, up).start()

    def arrived(l, slot):
        pltpu.make_async_remote_copy(
            blocks.at[l, slot], blocks.at[l, slot], send_cross.at[l, z], recv2.at[l, slot],
            device_id={"path": me + 1 - 2 * core}, device_id_type=MESH,
        ).wait_recv()

    def relay(l, d):
        @pl.when(z - d >= 0)
        def _():
            arrived(l, 2 * (z - d) + core)
            send_along(l, z - d, True)
            cross_copy(l, z - d).start()

        @pl.when(z + d < chips)
        def _():
            arrived(l, 2 * (z + d) + core)
            send_along(l, z + d, False)
            cross_copy(l, z + d).start()

    def finish_level(l):
        for owner in range(chips):
            arrived(l, 2 * owner + 1 - core)
        upper = routes[l, me] == 1
        for slot in range(n):
            gathered[l, :, slot * cols : (slot + 1) * cols] = jnp.where(upper, blocks[l, slot, 1], blocks[l, slot, 0])
        copy = pltpu.make_async_copy(gathered.at[l], path_out.at[0, l], store_sem.at[3, l])
        copy.start()
        stores.append(copy)

    def update_level(l):
        total = part[l]
        for k in range(1, n):
            path_copy(l, k, 1).wait_recv()
            total = total + part_in[l, lax.rem(me + k, n)]
        mean = jnp.sum(total, axis=1, keepdims=True) / entries
        factor = jnp.minimum(1.0, clip_rms / jnp.sqrt(mean + epsilon_sq))
        narrow = []
        for m in range(2):
            skipped = skips[m, l] > 0
            clipped = factor[m : m + 1, :] * average[l, m]
            momentum = mom[l, m]
            old = params[l, m]
            momentum = jnp.where(skipped, momentum, momentum_coef * momentum + clipped)
            new = jnp.where(skipped, old, old - outer_rate * (clipped + momentum_coef * momentum))
            mom[l, m] = momentum
            params[l, m] = new
            narrow.append(new.astype(jnp.bfloat16))
        for m in range(2):
            blocks[l, me, m] = narrow[m]
        send_along(l, z, True)
        send_along(l, z, False)
        cross_copy(l, z).start()
        for index, (src, dst) in enumerate(((mom, mom_out), (params, params_out))):
            copy = pltpu.make_async_copy(src.at[l], dst.at[l], store_sem.at[1 + index, l])
            copy.start()
            stores.append(copy)

    for l in range(min(ahead, levels)):
        send_level(l)
    for l in range(min(ahead, levels)):
        feedback_level(l)
    load_params.wait()
    load_mom.wait()
    for step in range(levels + 2 + chips):
        for d in range(chips - 1, 0, -1):
            if 0 <= step - 1 - d < levels:
                relay(step - 1 - d, d)
        if step < levels:
            reduce_level(step)
            share_level(step)
        if 0 <= step - 1 < levels:
            update_level(step - 1)
        if step + ahead < levels:
            send_level(step + ahead)
            feedback_level(step + ahead)
        if 0 <= step - 1 - chips < levels:
            finish_level(step - 1 - chips)

    for l in range(levels):
        for k in range(1, n):
            waiting1(l, k).wait_send()
            path_copy(l, k, 1).wait_send()
        for k in range(1, f):
            fsdp_copy(l, k, 1).wait_send()
        for owner in range(chips):
            cross_copy(l, owner).wait_send()

            @pl.when((owner <= z) & (z + 1 < chips))
            def _():
                along_copy(l, owner, True).wait_send()

            @pl.when((owner >= z) & (z > 0))
            def _():
                along_copy(l, owner, False).wait_send()

    for copy in stores:
        copy.wait()


def on_device(n, f, path_delta, feedback, global_params, momentum, routes, token_counts, skip_flags):
    _, levels, rows, depth = path_delta.shape
    cols = depth // n
    smem = pl.BlockSpec(memory_space=pltpu.SMEM)
    anywhere = pl.BlockSpec(memory_space=pl.ANY)
    shape = jax.ShapeDtypeStruct
    dma = pltpu.SemaphoreType.DMA
    bf16, f32 = jnp.bfloat16, jnp.float32
    return pl.pallas_call(
        functools.partial(kernel, n, f),
        out_shape=(
            shape(feedback.shape, f32),
            shape(momentum.shape, f32),
            shape(global_params.shape, f32),
            shape(path_delta.shape, bf16),
        ),
        in_specs=[smem] * 3 + [anywhere] * 4,
        out_specs=(anywhere,) * 4,
        scratch_shapes=[
            pltpu.VMEM((levels, rows, depth), bf16),
            pltpu.VMEM((levels, rows, depth), f32),
            pltpu.VMEM(global_params.shape, f32),
            pltpu.VMEM(global_params.shape, f32),
            pltpu.VMEM((levels, rows, depth), bf16),
            pltpu.VMEM((levels, n, rows, cols), bf16),
            pltpu.VMEM(global_params.shape, f32),
            pltpu.VMEM((levels, n, 2, rows, cols), bf16),
            pltpu.VMEM((levels, rows, depth), bf16),
            pltpu.VMEM((levels, 2, 128), f32),
            pltpu.VMEM((levels, f, 2, 128), f32),
            pltpu.VMEM((levels, 2, 128), f32),
            pltpu.VMEM((levels, n, 2, 128), f32),
            dma((4, levels)),
            dma((4, levels)),
            dma((levels, n)),
            dma((levels, n)),
            dma((levels, n // 2)),
            dma((levels, n // 2)),
            dma((levels, n // 2)),
            dma((levels, n)),
            dma((levels, f)),
            dma((levels, f)),
            dma((levels, n)),
            dma((levels, n)),
        ],
        compiler_params=pltpu.CompilerParams(collective_id=0, has_side_effects=True),
    )(routes.T, token_counts.T, skip_flags.T, path_delta, feedback, global_params, momentum)


def solution(mesh):
    return jax.shard_map(
        functools.partial(on_device, mesh.shape["path"], mesh.shape["fsdp"]),
        mesh=mesh,
        in_specs=(
            P("path", None, "fsdp", None),
            P("path", None, "fsdp", None),
            P(None, None, "fsdp", "path"),
            P(None, None, "fsdp", "path"),
            P(),
            P(),
            P(),
        ),
        out_specs=(
            P("path", None, "fsdp", None),
            P(None, None, "fsdp", "path"),
            P(None, None, "fsdp", "path"),
            P("path", None, "fsdp", None),
        ),
        check_vma=False,
    )
```

```python
import functools

import jax
import jax.numpy as jnp
from jax import lax
from jax.experimental import pallas as pl
from jax.experimental.pallas import tpu as pltpu
from jax.sharding import PartitionSpec as P

clip_rms = 0.2
outer_rate = 0.7
momentum_coef = 0.9
epsilon_sq = 1e-06
MESH = pl.DeviceIdType.MESH
ahead = 2


def kernel(
    n, f,
    routes, counts, skips, delta_hbm, feed_hbm, params_hbm, mom_hbm,
    feed_out, mom_out, params_out, path_out,
    delta, feed, params, mom, sent, recv, average, blocks, gathered,
    square, square_in, part, part_in,
    load_sem, store_sem, send1, recv1, send_up, send_down, send_cross, recv2, sendf, recvf, sendp, recvp,
):
    levels, rows, depth = delta.shape
    cols = depth // n
    me = lax.axis_index("path")
    mf = lax.axis_index("fsdp")
    entries = rows * cols * n * f

    loads = []
    for l in range(levels):
        pair = (
            pltpu.make_async_copy(delta_hbm.at[0, l], delta.at[l], load_sem.at[0, l]),
            pltpu.make_async_copy(feed_hbm.at[0, l], feed.at[l], load_sem.at[1, l]),
        )
        for copy in pair:
            copy.start()
        loads.append(pair)
    load_params = pltpu.make_async_copy(params_hbm, params, load_sem.at[2, 0])
    load_mom = pltpu.make_async_copy(mom_hbm, mom, load_sem.at[3, 0])
    load_params.start()
    load_mom.start()

    barrier = pltpu.get_barrier_semaphore()
    for k in range(1, n):
        pl.semaphore_signal(barrier, inc=1, device_id={"path": lax.rem(me + k, n)}, device_id_type=MESH)
    for k in range(1, f):
        pl.semaphore_signal(barrier, inc=1, device_id={"fsdp": lax.rem(mf + k, f)}, device_id_type=MESH)

    inverse = []
    stores = []

    def send_level(l):
        own_route = routes[l, me]
        total = jnp.int32(0)
        for q in range(n):
            total = total + jnp.where(routes[l, q] == own_route, counts[l, q], 0)
        live = 1 - jnp.where(own_route == 1, skips[1, l], skips[0, l])
        top = jnp.full((1, 128), (counts[l, me] * live).astype(jnp.float32))
        own = jnp.full((1, 128), counts[l, me].astype(jnp.float32))
        bottom = jnp.full((1, 128), total.astype(jnp.float32))
        weight = (top / bottom)[0:1, 0:1]
        inverse.append((bottom / own)[0:1, 0:1])
        for copy in loads[l]:
            copy.wait()
        for r in range(0, rows, 16):
            corrected = delta[l, r : r + 16, :].astype(jnp.float32) + feed[l, r : r + 16, :]
            sent[l, r : r + 16, :] = (weight * corrected).astype(jnp.bfloat16)
        if l == 0:
            pl.semaphore_wait(barrier, n - 1 + f - 1)
        for k in range(1, n):
            peer = lax.rem(me + k, n)
            pltpu.make_async_remote_copy(
                sent.at[l, :, pl.ds(pl.multiple_of(peer * cols, cols), cols)],
                recv.at[l, me],
                send1.at[l, k],
                recv1.at[l, me],
                device_id={"path": peer},
                device_id_type=MESH,
            ).start()

    def feedback_level(l):
        for r in range(0, rows, 16):
            corrected = delta[l, r : r + 16, :].astype(jnp.float32) + feed[l, r : r + 16, :]
            feed[l, r : r + 16, :] = corrected - sent[l, r : r + 16, :].astype(jnp.float32) * inverse[l]
        copy = pltpu.make_async_copy(feed.at[l], feed_out.at[0, l], store_sem.at[0, l])
        copy.start()
        stores.append(copy)

    mine = pl.ds(pl.multiple_of(me * cols, cols), cols)

    def waiting1(l, k):
        source = lax.rem(me + k, n)
        return pltpu.make_async_remote_copy(
            sent.at[l, :, pl.ds(pl.multiple_of(source * cols, cols), cols)],
            recv.at[l, source], send1.at[l, k], recv1.at[l, source],
            device_id={"path": source}, device_id_type=MESH,
        )

    def small(l, k, axis, at, size, src, dst, send, arrive, slot):
        peer = lax.rem(at + k, size)
        return pltpu.make_async_remote_copy(
            src.at[l], dst.at[l, at if slot is None else peer], send.at[l, k],
            arrive.at[l, at if slot is None else peer],
            device_id={axis: peer}, device_id_type=MESH,
        )

    fsdp_copy = lambda l, k, slot: small(l, k, "fsdp", mf, f, square, square_in, sendf, recvf, slot)
    path_copy = lambda l, k, slot: small(l, k, "path", me, n, part, part_in, sendp, recvp, slot)

    def reduce_level(l):
        for k in range(1, n):
            waiting1(l, k).wait_recv()
        own = sent[l, :, mine].astype(jnp.float32)
        own_upper = routes[l, me] == 1
        zero = jnp.zeros_like(own)
        first = jnp.where(own_upper, zero, own)
        second = jnp.where(own_upper, own, zero)
        for k in range(1, n):
            source = lax.rem(me + k, n)
            upper = routes[l, source] == 1
            block = recv[l, source].astype(jnp.float32)
            first = first + jnp.where(upper, zero, block)
            second = second + jnp.where(upper, block, zero)
        for m, value in enumerate((first, second)):
            average[l, m] = value
            lanes = jnp.sum(value * value, axis=0, keepdims=True)
            folded = lanes[:, 0:128]
            for c in range(128, cols, 128):
                folded = folded + lanes[:, c : c + 128]
            square[l, m : m + 1, :] = folded
        for k in range(1, f):
            fsdp_copy(l, k, None).start()

    def share_level(l):
        total = square[l]
        for k in range(1, f):
            fsdp_copy(l, k, 1).wait_recv()
            total = total + square_in[l, lax.rem(mf + k, f)]
        part[l] = total
        for k in range(1, n):
            path_copy(l, k, None).start()

    z, core = lax.div(me, 2), lax.rem(me, 2)
    chips = n // 2

    def along_copy(l, owner, up):
        slot = 2 * owner + core
        return pltpu.make_async_remote_copy(
            blocks.at[l, slot], blocks.at[l, slot],
            (send_up if up else send_down).at[l, owner], recv2.at[l, slot],
            device_id={"path": me + 2 if up else me - 2}, device_id_type=MESH,
        )

    def cross_copy(l, owner):
        slot = 2 * owner + core
        return pltpu.make_async_remote_copy(
            blocks.at[l, slot], blocks.at[l, slot], send_cross.at[l, owner], recv2.at[l, slot],
            device_id={"path": me + 1 - 2 * core}, device_id_type=MESH,
        )

    def send_along(l, owner, up):
        @pl.when(z + 1 < chips if up else z > 0)
        def _():
            along_copy(l, owner, up).start()

    def arrived(l, slot):
        pltpu.make_async_remote_copy(
            blocks.at[l, slot], blocks.at[l, slot], send_cross.at[l, z], recv2.at[l, slot],
            device_id={"path": me + 1 - 2 * core}, device_id_type=MESH,
        ).wait_recv()

    def relay(l, d):
        @pl.when(z - d >= 0)
        def _():
            arrived(l, 2 * (z - d) + core)
            send_along(l, z - d, True)
            cross_copy(l, z - d).start()

        @pl.when(z + d < chips)
        def _():
            arrived(l, 2 * (z + d) + core)
            send_along(l, z + d, False)
            cross_copy(l, z + d).start()

    def finish_level(l):
        for owner in range(chips):
            arrived(l, 2 * owner + 1 - core)
        upper = routes[l, me] == 1
        for slot in range(n):
            gathered[l, :, slot * cols : (slot + 1) * cols] = jnp.where(upper, blocks[l, slot, 1], blocks[l, slot, 0])
        copy = pltpu.make_async_copy(gathered.at[l], path_out.at[0, l], store_sem.at[3, l])
        copy.start()
        stores.append(copy)

    def update_level(l):
        total = part[l]
        for k in range(1, n):
            path_copy(l, k, 1).wait_recv()
            total = total + part_in[l, lax.rem(me + k, n)]
        mean = jnp.sum(total, axis=1, keepdims=True) / entries
        factor = jnp.minimum(1.0, clip_rms / jnp.sqrt(mean + epsilon_sq))
        narrow = []
        for m in range(2):
            skipped = skips[m, l] > 0
            clipped = factor[m : m + 1, :] * average[l, m]
            momentum = mom[l, m]
            old = params[l, m]
            momentum = jnp.where(skipped, momentum, momentum_coef * momentum + clipped)
            new = jnp.where(skipped, old, old - outer_rate * (clipped + momentum_coef * momentum))
            mom[l, m] = momentum
            params[l, m] = new
            narrow.append(new.astype(jnp.bfloat16))
        for m in range(2):
            blocks[l, me, m] = narrow[m]
        send_along(l, z, True)
        send_along(l, z, False)
        cross_copy(l, z).start()
        for index, (src, dst) in enumerate(((mom, mom_out), (params, params_out))):
            copy = pltpu.make_async_copy(src.at[l], dst.at[l], store_sem.at[1 + index, l])
            copy.start()
            stores.append(copy)

    for l in range(min(ahead, levels)):
        send_level(l)
    for l in range(min(ahead, levels)):
        feedback_level(l)
    load_params.wait()
    load_mom.wait()
    for step in range(levels + 1 + chips):
        if step < levels:
            reduce_level(step)
            share_level(step)
            if step + ahead < levels:
                send_level(step + ahead)
                feedback_level(step + ahead)
        if 0 <= step - 1 < levels:
            update_level(step - 1)
        for d in range(1, chips):
            if 0 <= step - 1 - d < levels:
                relay(step - 1 - d, d)
        if 0 <= step - 1 - chips < levels:
            finish_level(step - 1 - chips)

    for l in range(levels):
        for k in range(1, n):
            waiting1(l, k).wait_send()
            path_copy(l, k, 1).wait_send()
        for k in range(1, f):
            fsdp_copy(l, k, 1).wait_send()
        for owner in range(chips):
            cross_copy(l, owner).wait_send()

            @pl.when((owner <= z) & (z + 1 < chips))
            def _():
                along_copy(l, owner, True).wait_send()

            @pl.when((owner >= z) & (z > 0))
            def _():
                along_copy(l, owner, False).wait_send()

    for copy in stores:
        copy.wait()


def on_device(n, f, path_delta, feedback, global_params, momentum, routes, token_counts, skip_flags):
    _, levels, rows, depth = path_delta.shape
    cols = depth // n
    smem = pl.BlockSpec(memory_space=pltpu.SMEM)
    anywhere = pl.BlockSpec(memory_space=pl.ANY)
    shape = jax.ShapeDtypeStruct
    dma = pltpu.SemaphoreType.DMA
    bf16, f32 = jnp.bfloat16, jnp.float32
    return pl.pallas_call(
        functools.partial(kernel, n, f),
        out_shape=(
            shape(feedback.shape, f32),
            shape(momentum.shape, f32),
            shape(global_params.shape, f32),
            shape(path_delta.shape, bf16),
        ),
        in_specs=[smem] * 3 + [anywhere] * 4,
        out_specs=(anywhere,) * 4,
        scratch_shapes=[
            pltpu.VMEM((levels, rows, depth), bf16),
            pltpu.VMEM((levels, rows, depth), f32),
            pltpu.VMEM(global_params.shape, f32),
            pltpu.VMEM(global_params.shape, f32),
            pltpu.VMEM((levels, rows, depth), bf16),
            pltpu.VMEM((levels, n, rows, cols), bf16),
            pltpu.VMEM(global_params.shape, f32),
            pltpu.VMEM((levels, n, 2, rows, cols), bf16),
            pltpu.VMEM((levels, rows, depth), bf16),
            pltpu.VMEM((levels, 2, 128), f32),
            pltpu.VMEM((levels, f, 2, 128), f32),
            pltpu.VMEM((levels, 2, 128), f32),
            pltpu.VMEM((levels, n, 2, 128), f32),
            dma((4, levels)),
            dma((4, levels)),
            dma((levels, n)),
            dma((levels, n)),
            dma((levels, n // 2)),
            dma((levels, n // 2)),
            dma((levels, n // 2)),
            dma((levels, n)),
            dma((levels, f)),
            dma((levels, f)),
            dma((levels, n)),
            dma((levels, n)),
        ],
        compiler_params=pltpu.CompilerParams(collective_id=0, has_side_effects=True, vmem_limit_bytes=46 * 1024 * 1024),
    )(routes.T, token_counts.T, skip_flags.T, path_delta, feedback, global_params, momentum)


def solution(mesh):
    return jax.shard_map(
        functools.partial(on_device, mesh.shape["path"], mesh.shape["fsdp"]),
        mesh=mesh,
        in_specs=(
            P("path", None, "fsdp", None),
            P("path", None, "fsdp", None),
            P(None, None, "fsdp", "path"),
            P(None, None, "fsdp", "path"),
            P(),
            P(),
            P(),
        ),
        out_specs=(
            P("path", None, "fsdp", None),
            P(None, None, "fsdp", "path"),
            P(None, None, "fsdp", "path"),
            P("path", None, "fsdp", None),
        ),
        check_vma=False,
    )
```

```python
import functools

import jax
import jax.numpy as jnp
from jax import lax
from jax.experimental import pallas as pl
from jax.experimental.pallas import tpu as pltpu
from jax.sharding import PartitionSpec as P

clip_rms = 0.2
outer_rate = 0.7
momentum_coef = 0.9
epsilon_sq = 1e-06
MESH = pl.DeviceIdType.MESH
ahead = 3


def kernel(
    n, f,
    routes, counts, skips, delta_hbm, feed_hbm, params_hbm, mom_hbm,
    feed_out, mom_out, params_out, path_out,
    delta, feed, params, mom, sent, recv, average, blocks, gathered,
    square, square_in, part, part_in,
    load_sem, store_sem, send1, recv1, send_up, send_down, send_cross, recv2, sendf, recvf, sendp, recvp,
):
    levels, rows, depth = delta.shape
    cols = depth // n
    me = lax.axis_index("path")
    mf = lax.axis_index("fsdp")
    entries = rows * cols * n * f

    loads = []
    for l in range(levels):
        pair = (
            pltpu.make_async_copy(delta_hbm.at[0, l], delta.at[l], load_sem.at[0, l]),
            pltpu.make_async_copy(feed_hbm.at[0, l], feed.at[l], load_sem.at[1, l]),
        )
        for copy in pair:
            copy.start()
        loads.append(pair)
    load_params = pltpu.make_async_copy(params_hbm, params, load_sem.at[2, 0])
    load_mom = pltpu.make_async_copy(mom_hbm, mom, load_sem.at[3, 0])
    load_params.start()
    load_mom.start()

    barrier = pltpu.get_barrier_semaphore()
    for k in range(1, n):
        pl.semaphore_signal(barrier, inc=1, device_id={"path": lax.rem(me + k, n)}, device_id_type=MESH)
    for k in range(1, f):
        pl.semaphore_signal(barrier, inc=1, device_id={"fsdp": lax.rem(mf + k, f)}, device_id_type=MESH)

    inverse = []
    stores = []

    def send_level(l):
        own_route = routes[l, me]
        total = jnp.int32(0)
        for q in range(n):
            total = total + jnp.where(routes[l, q] == own_route, counts[l, q], 0)
        live = 1 - jnp.where(own_route == 1, skips[1, l], skips[0, l])
        top = jnp.full((1, 128), (counts[l, me] * live).astype(jnp.float32))
        own = jnp.full((1, 128), counts[l, me].astype(jnp.float32))
        bottom = jnp.full((1, 128), total.astype(jnp.float32))
        weight = (top / bottom)[0:1, 0:1]
        inverse.append((bottom / own)[0:1, 0:1])
        for copy in loads[l]:
            copy.wait()
        for r in range(0, rows, 16):
            corrected = delta[l, r : r + 16, :].astype(jnp.float32) + feed[l, r : r + 16, :]
            sent[l, r : r + 16, :] = (weight * corrected).astype(jnp.bfloat16)
        if l == 0:
            pl.semaphore_wait(barrier, n - 1 + f - 1)
        for k in range(1, n):
            peer = lax.rem(me + k, n)
            pltpu.make_async_remote_copy(
                sent.at[l, :, pl.ds(pl.multiple_of(peer * cols, cols), cols)],
                recv.at[l, me],
                send1.at[l, k],
                recv1.at[l, me],
                device_id={"path": peer},
                device_id_type=MESH,
            ).start()

    def feedback_level(l):
        for r in range(0, rows, 16):
            corrected = delta[l, r : r + 16, :].astype(jnp.float32) + feed[l, r : r + 16, :]
            feed[l, r : r + 16, :] = corrected - sent[l, r : r + 16, :].astype(jnp.float32) * inverse[l]
        copy = pltpu.make_async_copy(feed.at[l], feed_out.at[0, l], store_sem.at[0, l])
        copy.start()
        stores.append(copy)

    mine = pl.ds(pl.multiple_of(me * cols, cols), cols)

    def waiting1(l, k):
        source = lax.rem(me + k, n)
        return pltpu.make_async_remote_copy(
            sent.at[l, :, pl.ds(pl.multiple_of(source * cols, cols), cols)],
            recv.at[l, source], send1.at[l, k], recv1.at[l, source],
            device_id={"path": source}, device_id_type=MESH,
        )

    def small(l, k, axis, at, size, src, dst, send, arrive, slot):
        peer = lax.rem(at + k, size)
        return pltpu.make_async_remote_copy(
            src.at[l], dst.at[l, at if slot is None else peer], send.at[l, k],
            arrive.at[l, at if slot is None else peer],
            device_id={axis: peer}, device_id_type=MESH,
        )

    fsdp_copy = lambda l, k, slot: small(l, k, "fsdp", mf, f, square, square_in, sendf, recvf, slot)
    path_copy = lambda l, k, slot: small(l, k, "path", me, n, part, part_in, sendp, recvp, slot)

    def reduce_level(l):
        for k in range(1, n):
            waiting1(l, k).wait_recv()
        own = sent[l, :, mine].astype(jnp.float32)
        own_upper = routes[l, me] == 1
        zero = jnp.zeros_like(own)
        first = jnp.where(own_upper, zero, own)
        second = jnp.where(own_upper, own, zero)
        for k in range(1, n):
            source = lax.rem(me + k, n)
            upper = routes[l, source] == 1
            block = recv[l, source].astype(jnp.float32)
            first = first + jnp.where(upper, zero, block)
            second = second + jnp.where(upper, block, zero)
        for m, value in enumerate((first, second)):
            average[l, m] = value
            lanes = jnp.sum(value * value, axis=0, keepdims=True)
            folded = lanes[:, 0:128]
            for c in range(128, cols, 128):
                folded = folded + lanes[:, c : c + 128]
            square[l, m : m + 1, :] = folded
        for k in range(1, f):
            fsdp_copy(l, k, None).start()

    def share_level(l):
        total = square[l]
        for k in range(1, f):
            fsdp_copy(l, k, 1).wait_recv()
            total = total + square_in[l, lax.rem(mf + k, f)]
        part[l] = total
        for k in range(1, n):
            path_copy(l, k, None).start()

    z, core = lax.div(me, 2), lax.rem(me, 2)
    chips = n // 2

    def along_copy(l, owner, up):
        slot = 2 * owner + core
        return pltpu.make_async_remote_copy(
            blocks.at[l, slot], blocks.at[l, slot],
            (send_up if up else send_down).at[l, owner], recv2.at[l, slot],
            device_id={"path": me + 2 if up else me - 2}, device_id_type=MESH,
        )

    def cross_copy(l, owner):
        slot = 2 * owner + core
        return pltpu.make_async_remote_copy(
            blocks.at[l, slot], blocks.at[l, slot], send_cross.at[l, owner], recv2.at[l, slot],
            device_id={"path": me + 1 - 2 * core}, device_id_type=MESH,
        )

    def send_along(l, owner, up):
        @pl.when(z + 1 < chips if up else z > 0)
        def _():
            along_copy(l, owner, up).start()

    def arrived(l, slot):
        pltpu.make_async_remote_copy(
            blocks.at[l, slot], blocks.at[l, slot], send_cross.at[l, z], recv2.at[l, slot],
            device_id={"path": me + 1 - 2 * core}, device_id_type=MESH,
        ).wait_recv()

    def relay(l, d):
        @pl.when(z - d >= 0)
        def _():
            arrived(l, 2 * (z - d) + core)
            send_along(l, z - d, True)
            cross_copy(l, z - d).start()

        @pl.when(z + d < chips)
        def _():
            arrived(l, 2 * (z + d) + core)
            send_along(l, z + d, False)
            cross_copy(l, z + d).start()

    def finish_level(l):
        for owner in range(chips):
            arrived(l, 2 * owner + 1 - core)
        upper = routes[l, me] == 1
        for slot in range(n):
            gathered[l, :, slot * cols : (slot + 1) * cols] = jnp.where(upper, blocks[l, slot, 1], blocks[l, slot, 0])
        copy = pltpu.make_async_copy(gathered.at[l], path_out.at[0, l], store_sem.at[3, l])
        copy.start()
        stores.append(copy)

    def update_level(l):
        total = part[l]
        for k in range(1, n):
            path_copy(l, k, 1).wait_recv()
            total = total + part_in[l, lax.rem(me + k, n)]
        mean = jnp.sum(total, axis=1, keepdims=True) / entries
        factor = jnp.minimum(1.0, clip_rms / jnp.sqrt(mean + epsilon_sq))
        narrow = []
        for m in range(2):
            skipped = skips[m, l] > 0
            clipped = factor[m : m + 1, :] * average[l, m]
            momentum = mom[l, m]
            old = params[l, m]
            momentum = jnp.where(skipped, momentum, momentum_coef * momentum + clipped)
            new = jnp.where(skipped, old, old - outer_rate * (clipped + momentum_coef * momentum))
            mom[l, m] = momentum
            params[l, m] = new
            narrow.append(new.astype(jnp.bfloat16))
        for m in range(2):
            blocks[l, me, m] = narrow[m]
        send_along(l, z, True)
        send_along(l, z, False)
        cross_copy(l, z).start()
        for index, (src, dst) in enumerate(((mom, mom_out), (params, params_out))):
            copy = pltpu.make_async_copy(src.at[l], dst.at[l], store_sem.at[1 + index, l])
            copy.start()
            stores.append(copy)

    for l in range(min(ahead, levels)):
        send_level(l)
    for l in range(min(ahead, levels)):
        feedback_level(l)
    load_params.wait()
    load_mom.wait()
    for step in range(levels + 1 + chips):
        if step < levels:
            reduce_level(step)
            share_level(step)
            if step + ahead < levels:
                send_level(step + ahead)
                feedback_level(step + ahead)
        if 0 <= step - 1 < levels:
            update_level(step - 1)
        for d in range(1, chips):
            if 0 <= step - 1 - d < levels:
                relay(step - 1 - d, d)
        if 0 <= step - 1 - chips < levels:
            finish_level(step - 1 - chips)

    for l in range(levels):
        for k in range(1, n):
            waiting1(l, k).wait_send()
            path_copy(l, k, 1).wait_send()
        for k in range(1, f):
            fsdp_copy(l, k, 1).wait_send()
        for owner in range(chips):
            cross_copy(l, owner).wait_send()

            @pl.when((owner <= z) & (z + 1 < chips))
            def _():
                along_copy(l, owner, True).wait_send()

            @pl.when((owner >= z) & (z > 0))
            def _():
                along_copy(l, owner, False).wait_send()

    for copy in stores:
        copy.wait()


def on_device(n, f, path_delta, feedback, global_params, momentum, routes, token_counts, skip_flags):
    _, levels, rows, depth = path_delta.shape
    cols = depth // n
    smem = pl.BlockSpec(memory_space=pltpu.SMEM)
    anywhere = pl.BlockSpec(memory_space=pl.ANY)
    shape = jax.ShapeDtypeStruct
    dma = pltpu.SemaphoreType.DMA
    bf16, f32 = jnp.bfloat16, jnp.float32
    return pl.pallas_call(
        functools.partial(kernel, n, f),
        out_shape=(
            shape(feedback.shape, f32),
            shape(momentum.shape, f32),
            shape(global_params.shape, f32),
            shape(path_delta.shape, bf16),
        ),
        in_specs=[smem] * 3 + [anywhere] * 4,
        out_specs=(anywhere,) * 4,
        scratch_shapes=[
            pltpu.VMEM((levels, rows, depth), bf16),
            pltpu.VMEM((levels, rows, depth), f32),
            pltpu.VMEM(global_params.shape, f32),
            pltpu.VMEM(global_params.shape, f32),
            pltpu.VMEM((levels, rows, depth), bf16),
            pltpu.VMEM((levels, n, rows, cols), bf16),
            pltpu.VMEM(global_params.shape, f32),
            pltpu.VMEM((levels, n, 2, rows, cols), bf16),
            pltpu.VMEM((levels, rows, depth), bf16),
            pltpu.VMEM((levels, 2, 128), f32),
            pltpu.VMEM((levels, f, 2, 128), f32),
            pltpu.VMEM((levels, 2, 128), f32),
            pltpu.VMEM((levels, n, 2, 128), f32),
            dma((4, levels)),
            dma((4, levels)),
            dma((levels, n)),
            dma((levels, n)),
            dma((levels, n // 2)),
            dma((levels, n // 2)),
            dma((levels, n // 2)),
            dma((levels, n)),
            dma((levels, f)),
            dma((levels, f)),
            dma((levels, n)),
            dma((levels, n)),
        ],
        compiler_params=pltpu.CompilerParams(collective_id=0, has_side_effects=True),
    )(routes.T, token_counts.T, skip_flags.T, path_delta, feedback, global_params, momentum)


def solution(mesh):
    return jax.shard_map(
        functools.partial(on_device, mesh.shape["path"], mesh.shape["fsdp"]),
        mesh=mesh,
        in_specs=(
            P("path", None, "fsdp", None),
            P("path", None, "fsdp", None),
            P(None, None, "fsdp", "path"),
            P(None, None, "fsdp", "path"),
            P(),
            P(),
            P(),
        ),
        out_specs=(
            P("path", None, "fsdp", None),
            P(None, None, "fsdp", "path"),
            P(None, None, "fsdp", "path"),
            P("path", None, "fsdp", None),
        ),
        check_vma=False,
    )
```
